32 devices in a mesh: gz: 2 (over x), gy: 4 (over z), gx: 4 (over y, core).
Axes of the slice: x: 2, y: 2, z: 4, core: 2. Of those that a mesh axis runs over, the one named last changes fastest.
Arguments:
- density: float32 [16, 32, 512], P('gz', 'gy', 'gx'), may hold values from 0.3 to 3
- velocity: float32 [3, 16, 32, 512], P(None, 'gz', 'gy', 'gx'), may hold values from -3 to 3
- pressure: float32 [16, 32, 512], P('gz', 'gy', 'gx'), may hold values from 0.3 to 3
- field: float32 [3, 16, 32, 512], P(None, 'gz', 'gy', 'gx'), may hold values from -3 to 3
- corona: int32 [16], replicated, may hold values from 0 to 1, as said below
Outputs:
- conserved: float32 [5, 16, 32, 512], P(None, 'gz', 'gy', 'gx')
- faces_new: float32 [3, 16, 32, 512], P(None, 'gz', 'gy', 'gx')
The draws below stay inside these ranges and needn't reach their ends.
Inputs may be any that keep to these rules, and one draw needn't show every extreme that they name: `corona`: 1 marks a cooled slab; every slab farther from the midplane than a drawn height (one for each half of z) is cooled, and some other slabs are cooled too.
All inputs are finite; a program needn't handle non-finite values.
Results may differ from the reference program's by a relative error of at most 0.00002.
Values sent between devices are 32-bit elements; how exact they have to be, the bound alone decides.
A program may use at most 64 MiB of HBM per device.

```python
import math
import jax
import jax.numpy as jnp

COOL_STEPS = 8
NX = 512
NY = 32
NZ = 16


def draw_corona(key, part):
    lower_key = jax.random.fold_in(key, 11)
    upper_key = jax.random.fold_in(key, 23)
    extra_key = jax.random.fold_in(key, 37)
    lower_height = jax.random.randint(lower_key, (), NZ // 4, 3 * NZ // 8 + 1)
    upper_height = jax.random.randint(upper_key, (), NZ // 4, 3 * NZ // 8 + 1)
    index = jnp.arange(NZ, dtype=jnp.int32)
    offsets = jnp.abs(2 * index + 1 - NZ)
    threshold = jnp.where(2 * index < NZ, lower_height, upper_height)
    outer = offsets > 2 * threshold
    extra = jax.random.randint(extra_key, (NZ,), 0, 4) == 0
    return jnp.logical_or(outer, extra).astype(jnp.int32)


def shard_levels(own_key, dims, split, least, largest):
    def one(axis_at, shards_of):
        draws = jax.random.uniform(jax.random.fold_in(jax.random.fold_in(own_key, 6), axis_at), (shards_of,), jnp.float32, least / len(split), largest / len(split))
        return jnp.repeat(jnp.exp(draws), dims[axis_at] // shards_of).reshape((-1,) + (1,) * (len(dims) - axis_at - 1))

    level = one(*split[0])
    for cut in split[1:]:
        level = level * one(*cut)
    return level


def noise(stream_key, extent, scale, limit, cuts=(), kind=jnp.bfloat16):
    level = shard_levels(stream_key, extent, cuts, -0.22, 0.18) if cuts else 1.0
    values = jax.random.normal(stream_key, extent, jnp.float32) * scale * level
    return jnp.minimum(jnp.maximum(values, -limit), limit).astype(kind)


def setup_inputs(seed: int = 0) -> dict:
    splits = jax.random.split(jax.random.key(seed), 6)
    density = jnp.clip(jnp.exp(math.log(3.0) - 2.3025851 * jax.random.uniform(splits[0], (NZ, NY, NX), jnp.float32) ** shard_levels(splits[0], (NZ, NY, NX), ((0, 2), (1, 4), (2, 4)), -0.2, 0.2)), 0.3, 3.0)
    velocity = noise(splits[1], (3, NZ, NY, NX), 0.5, 3.0, ((1, 2), (2, 4), (3, 4)), jnp.float32)
    pressure = jnp.clip(jnp.exp(math.log(3.0) - 2.3025851 * jax.random.uniform(splits[2], (NZ, NY, NX), jnp.float32) ** shard_levels(splits[2], (NZ, NY, NX), ((0, 2), (1, 4), (2, 4)), -0.2, 0.2)), 0.3, 3.0)
    field = noise(splits[3], (3, NZ, NY, NX), 0.5, 3.0, ((1, 2), (2, 4), (3, 4)), jnp.float32)
    corona = draw_corona(jax.random.fold_in(splits[5], 71), 0)
    return {"density": density, "velocity": velocity, "pressure": pressure, "field": field, "corona": corona}


adiabatic = 5.0 / 3.0
courant = 0.08
cool_rate = 0.03
gravity = 1.0
cyclic_pairs = ((2, 1), (0, 2), (1, 0))

def shift_up(values, along):
    return jnp.roll(values, -1, along)

def shift_down(values, along):
    return jnp.roll(values, 1, along)

def cool_cells(density, pressure):
    for subcycle in range(COOL_STEPS):
        pressure = pressure / (1.0 + cool_rate * jnp.sqrt(density * pressure))
    return pressure

def state_terms(density, velocity, pressure, magnetic, normal_axis):
    others = [component for component in range(3) if component != normal_axis]
    normal_field = magnetic[normal_axis]
    transverse = magnetic[others[0]] * magnetic[others[0]] + magnetic[others[1]] * magnetic[others[1]]
    squared = transverse + normal_field * normal_field
    total_pressure = pressure + 0.5 * squared
    kinetic = velocity[0] * velocity[0] + velocity[1] * velocity[1] + velocity[2] * velocity[2]
    alignment = velocity[0] * magnetic[0] + velocity[1] * magnetic[1] + velocity[2] * magnetic[2]
    energy = pressure / (adiabatic - 1.0) + 0.5 * density * kinetic + 0.5 * squared
    sound = adiabatic * pressure / density
    along_field = normal_field * normal_field / density
    across_field = transverse / density
    fast_speed = jnp.sqrt(0.5 * (sound + along_field + across_field + jnp.sqrt((sound - along_field - across_field) ** 2 + 4.0 * sound * across_field)))
    normal_speed = velocity[normal_axis]
    conserved = [density] + [density * velocity[component] for component in range(3)] + [energy] + [magnetic[component] for component in others]
    fluxes = [density * normal_speed]
    for component in range(3):
        moment = density * velocity[component] * normal_speed - magnetic[component] * normal_field
        if component == normal_axis:
            moment = moment + total_pressure
        fluxes.append(moment)
    fluxes.append((energy + total_pressure) * normal_speed - normal_field * alignment)
    for component in others:
        fluxes.append(normal_speed * magnetic[component] - velocity[component] * normal_field)
    return (normal_speed, fast_speed, conserved, fluxes)

def interface_flux(density, velocity, pressure, centre, normal_face, normal_axis):
    lower_field = [shift_down(member, normal_axis) for member in centre]
    lower_field[normal_axis] = normal_face
    upper_field = list(centre)
    upper_field[normal_axis] = normal_face
    lower_terms = state_terms(shift_down(density, normal_axis), [shift_down(member, normal_axis) for member in velocity], shift_down(pressure, normal_axis), lower_field, normal_axis)
    upper_terms = state_terms(density, velocity, pressure, upper_field, normal_axis)
    slowest = jnp.minimum(jnp.minimum(lower_terms[0] - lower_terms[1], upper_terms[0] - upper_terms[1]), 0.0)
    fastest = jnp.maximum(jnp.maximum(lower_terms[0] + lower_terms[1], upper_terms[0] + upper_terms[1]), 0.0)
    inverse = 1.0 / (fastest - slowest)
    result = []
    for member in range(7):
        lower_flux = lower_terms[3][member]
        upper_flux = upper_terms[3][member]
        jump = upper_terms[2][member] - lower_terms[2][member]
        result.append((fastest * lower_flux - slowest * upper_flux + slowest * fastest * jump) * inverse)
    return result

def advance(extended, height):
    density = extended[0]
    velocity = [extended[1], extended[2], extended[3]]
    pressure = extended[4]
    faces = [extended[5], extended[6], extended[7]]
    centre = [0.5 * (faces[component] + shift_up(faces[component], component)) for component in range(3)]
    fluxes = [interface_flux(density, velocity, pressure, centre, faces[direction], direction) for direction in range(3)]
    kinetic = velocity[0] * velocity[0] + velocity[1] * velocity[1] + velocity[2] * velocity[2]
    squared = centre[0] * centre[0] + centre[1] * centre[1] + centre[2] * centre[2]
    energy = pressure / (adiabatic - 1.0) + 0.5 * density * kinetic + 0.5 * squared
    conserved = [density, density * velocity[0], density * velocity[1], density * velocity[2], energy]
    inner = (slice(2, -2), slice(2, -2), slice(2, -2))
    updated = []
    for member in range(5):
        change = jnp.zeros_like(density)
        for direction in range(3):
            change = change + shift_up(fluxes[direction][member], direction) - fluxes[direction][member]
        updated.append((conserved[member] - courant * change)[inner])
    pull = -gravity * height[:, None, None]
    updated[1] = updated[1] + courant * density[inner] * pull
    updated[4] = updated[4] + courant * density[inner] * velocity[0][inner] * pull
    electric = []
    for edge in range(3):
        first, second = cyclic_pairs[edge]
        first_others = [component for component in range(3) if component != first]
        second_others = [component for component in range(3) if component != second]
        first_flux = fluxes[first][5 + first_others.index(second)]
        second_flux = fluxes[second][5 + second_others.index(first)]
        electric.append(0.25 * (second_flux + shift_down(second_flux, first) - first_flux - shift_down(first_flux, second)))
    new_faces = []
    for component in range(3):
        across, beyond = cyclic_pairs[component]
        curl = shift_up(electric[beyond], across) - electric[beyond] - (shift_up(electric[across], beyond) - electric[across])
        new_faces.append((faces[component] - courant * curl)[inner])
    return (jnp.stack(updated), jnp.stack(new_faces))

def reference(density, velocity, pressure, field, corona):
    cooled = jnp.where(corona[:, None, None] == 1, cool_cells(density, pressure), pressure)
    stacked = jnp.concatenate([density[None], velocity, cooled[None], field], 0)
    extended = jnp.pad(stacked, ((0, 0), (0, 0), (0, 0), (2, 2)), mode='wrap')
    extended = jnp.pad(extended, ((0, 0), (0, 0), (2, 2), (0, 0)), mode='edge')
    extended = jnp.pad(extended, ((0, 0), (2, 2), (0, 0), (0, 0)), mode='edge')
    height = (2 * jnp.arange(NZ, dtype=jnp.int32) + 1 - NZ).astype(jnp.float32) / NZ
    return advance(extended, height)
```

```python
import functools

import jax
import jax.numpy as jnp
from jax import lax
from jax.experimental import pallas as pl
from jax.experimental.pallas import tpu as pltpu
from jax.sharding import PartitionSpec as P

COOL_STEPS = 8
adiabatic = 5.0 / 3.0
courant = 0.08
cool_rate = 0.03
gravity = 1.0

MESH = pl.DeviceIdType.MESH
DIRS = ((0, -1), (0, 1), (-1, 0), (1, 0), (-1, -1), (-1, 1), (1, -1), (1, 1))
FIELDS = 8
FZ, FY, FX = 5, 6, 7
PARTS = 15


def fast_speed(sound, normal_sq, transverse_sq, inv_rho):
    along = normal_sq * inv_rho
    across = transverse_sq * inv_rho
    gap = sound - along - across
    return jnp.sqrt(0.5 * (sound + along + across + jnp.sqrt(gap * gap + 4.0 * sound * across)))


def state_terms(cell, velocity, pressure, magnetic, axis):
    rho, inv_rho, sound, hydro, momenta = cell
    others = [c for c in range(3) if c != axis]
    normal = magnetic[axis]
    normal_sq = normal * normal
    transverse_sq = magnetic[others[0]] * magnetic[others[0]] + magnetic[others[1]] * magnetic[others[1]]
    squared = transverse_sq + normal_sq
    half = 0.5 * squared
    total = pressure + half
    energy = hydro + half
    align = velocity[0] * magnetic[0] + velocity[1] * magnetic[1] + velocity[2] * magnetic[2]
    speed = fast_speed(sound, normal_sq, transverse_sq, inv_rho)
    va = velocity[axis]
    conserved = [rho] + list(momenta) + [energy] + [magnetic[c] for c in others]
    fluxes = [momenta[axis]]
    for c in range(3):
        moment = momenta[c] * va - magnetic[c] * normal
        if c == axis:
            moment = moment + total
        fluxes.append(moment)
    fluxes.append((energy + total) * va - normal * align)
    for c in others:
        fluxes.append(va * magnetic[c] - velocity[c] * normal)
    return va, speed, conserved, fluxes


def cell_terms(rho, velocity, pressure):
    inv_rho = 1.0 / rho
    momenta = [rho * v for v in velocity]
    kinetic = momenta[0] * velocity[0] + momenta[1] * velocity[1] + momenta[2] * velocity[2]
    hydro = pressure * (1.0 / (adiabatic - 1.0)) + 0.5 * kinetic
    return rho, inv_rho, adiabatic * pressure * inv_rho, hydro, momenta


def hll(lower, upper):
    slow = jnp.minimum(jnp.minimum(lower[0] - lower[1], upper[0] - upper[1]), 0.0)
    fast = jnp.maximum(jnp.maximum(lower[0] + lower[1], upper[0] + upper[1]), 0.0)
    inverse = 1.0 / (fast - slow)
    wl = fast * inverse
    wu = -slow * inverse
    wj = slow * wl
    return [
        wl * lower[3][m] + wu * upper[3][m] + wj * (upper[2][m] - lower[2][m]) for m in range(7)
    ]


def kernel(
    sizes, rho_ref, vel_ref, pre_ref, fld_ref, corona_ref, cons_ref, face_ref,
    cooled, sbuf, rbuf, pad, ext, part, res, send_sem, recv_sem,
):
    nz, ny, nx, gz, gy, gx = sizes
    plane = nz * ny
    wide = ny + 3
    iz, iy, ix = lax.axis_index("gz"), lax.axis_index("gy"), lax.axis_index("gx")
    left = lax.rem(ix + gx - 1, gx)
    right = lax.rem(ix + 1, gx)

    has = {-1: {}, 1: {}}
    has_z = {-1: iz > 0, 0: None, 1: iz < gz - 1}
    has_y = {-1: iy > 0, 0: None, 1: iy < gy - 1}

    def exists(dz, dy):
        if dz == 0:
            return has_y[dy]
        if dy == 0:
            return has_z[dz]
        return jnp.logical_and(has_z[dz], has_y[dy])

    barrier = pltpu.get_barrier_semaphore()
    for to in (left, right):
        pl.semaphore_signal(barrier, inc=1, device_id={"gx": to}, device_id_type=MESH)
    for dz, dy in DIRS:
        @pl.when(exists(dz, dy))
        def _():
            pl.semaphore_signal(
                barrier, inc=1, device_id={"gz": iz + dz, "gy": iy + dy}, device_id_type=MESH
            )

    for z in range(nz):
        rows = pl.ds(z * ny, ny)
        rho = rho_ref[rows, :]
        start = pre_ref[rows, :]
        p = start
        for _ in range(COOL_STEPS):
            p = p / (1.0 + cool_rate * jnp.sqrt(rho * p))
        mark = jnp.full(p.shape, corona_ref[iz * nz + z], jnp.int32)
        cooled[rows, :] = jnp.where(mark == 1, p, start)

    sources = (
        [(rho_ref, 0)] + [(vel_ref, c * plane) for c in range(3)] + [(cooled, 0)]
        + [(fld_ref, c * plane) for c in range(3)]
    )

    def y_rows(f, y):
        ref, base = sources[f]
        return ref[pl.ds(base + y, nz, stride=ny), :]

    def z_rows(f, z):
        ref, base = sources[f]
        return ref[pl.ds(base + z * ny, ny), :]

    def one_row(f, z, y):
        ref, base = sources[f]
        return ref[pl.ds(base + z * ny + y, 1), :]

    zf, yf = FIELDS * ny, FIELDS * nz
    for f in range(FIELDS):
        for d, at in ((0, 0), (1, ny - 1)):
            sbuf[d, pl.ds(f * nz, nz), :] = y_rows(f, at)
        for d, at in ((2, 0), (3, nz - 1)):
            sbuf[d, pl.ds(f * ny, ny), :] = z_rows(f, at)
        for d in range(4, 8):
            dz, dy = DIRS[d]
            sbuf[d, pl.ds(f, 1), :] = one_row(f, 0 if dz < 0 else nz - 1, 0 if dy < 0 else ny - 1)
    sbuf[0, pl.ds(yf, nz), :] = y_rows(FY, 1)
    sbuf[2, pl.ds(zf, ny), :] = z_rows(FZ, 1)
    sbuf[5, pl.ds(FIELDS, 1), :] = one_row(FZ, 1, ny - 1)
    sbuf[6, pl.ds(FIELDS, 1), :] = one_row(FY, nz - 1, 1)
    size = (yf + nz, yf, zf + ny, zf, 16, 16, 16, 16)

    for f in range(FIELDS):
        for z in range(nz):
            pad[pl.ds(f * 128 + (z + 1) * wide + 1, ny), :] = z_rows(f, z)

    pl.semaphore_wait(
        barrier,
        2 + sum(exists(dz, dy).astype(jnp.int32) for dz, dy in DIRS),
    )

    def message(d):
        dz, dy = DIRS[d]
        return pltpu.make_async_remote_copy(
            src_ref=sbuf.at[d, pl.ds(0, size[d])],
            dst_ref=rbuf.at[d, pl.ds(0, size[d])],
            send_sem=send_sem.at[d],
            recv_sem=recv_sem.at[d],
            device_id={"gz": iz + dz, "gy": iy + dy},
            device_id_type=MESH,
        )

    for d in (4, 5, 6, 7, 0, 1, 2, 3):
        @pl.when(exists(*DIRS[d]))
        def _():
            message(d).start()

    for d in range(4):
        dz, dy = DIRS[d]
        own = DIRS.index((-dz, -dy))
        step = nz if dz == 0 else ny

        @pl.when(jnp.logical_not(exists(-dz, -dy)))
        def _():
            for f in range(FIELDS):
                rbuf[d, pl.ds(f * step, step), :] = sbuf[own, pl.ds(f * step, step), :]
            if dz + dy < 0:
                f = FY if dz == 0 else FZ
                rbuf[d, pl.ds(FIELDS * step, step), :] = sbuf[own, pl.ds(f * step, step), :]

    for d in range(8):
        dz, dy = DIRS[d]

        @pl.when(exists(-dz, -dy))
        def _():
            message(d).wait_recv()

    for f in range(FIELDS):
        base = f * 128
        pad[pl.ds(base + wide, nz, stride=wide), :] = rbuf[1, pl.ds(f * nz, nz), :]
        pad[pl.ds(base + wide + ny + 1, nz, stride=wide), :] = rbuf[0, pl.ds(f * nz, nz), :]
        pad[pl.ds(base + 1, ny), :] = rbuf[3, pl.ds(f * ny, ny), :]
        pad[pl.ds(base + (nz + 1) * wide + 1, ny), :] = rbuf[2, pl.ds(f * ny, ny), :]
    pad[pl.ds(FY * 128 + wide + ny + 2, nz, stride=wide), :] = rbuf[0, pl.ds(yf, nz), :]
    pad[pl.ds(FZ * 128 + (nz + 2) * wide + 1, ny), :] = rbuf[2, pl.ds(zf, ny), :]

    def spot(z, y):
        return (z + 1) * wide + y + 1

    for d in range(4, 8):
        dz, dy = DIRS[d]
        zg, yg = (nz if dz < 0 else -1), (ny if dy < 0 else -1)
        zc, yc = min(max(zg, 0), nz - 1), min(max(yg, 0), ny - 1)
        both = exists(-dz, -dy)
        extra = {5: (FZ, 1, 0), 6: (FY, 0, 1)}.get(d)

        @pl.when(both)
        def _():
            pad[pl.ds(spot(zg, yg), FIELDS, stride=128), :] = rbuf[d, pl.ds(0, FIELDS), :]
            if extra:
                f, ez, ey = extra
                pad[pl.ds(f * 128 + spot(zg + ez, yg + ey), 1), :] = rbuf[d, pl.ds(FIELDS, 1), :]

        def copy_rows(zs, ys):
            pad[pl.ds(spot(zg, yg), FIELDS, stride=128), :] = pad[
                pl.ds(spot(zs, ys), FIELDS, stride=128), :
            ]

        @pl.when(jnp.logical_not(has_z[-dz]))
        def _():
            copy_rows(zc, yg)
            if extra:
                f, ez, ey = extra
                pad[pl.ds(f * 128 + spot(zg + ez, yg + ey), 1), :] = pad[
                    pl.ds(f * 128 + spot(zc, yg + ey), 1), :
                ]

        @pl.when(jnp.logical_and(has_z[-dz], jnp.logical_not(has_y[-dy])))
        def _():
            copy_rows(zg, yc)
            if extra:
                f, ez, ey = extra
                pad[pl.ds(f * 128 + spot(zg + ez, yg + ey), 1), :] = pad[
                    pl.ds(f * 128 + spot(zg + ez, yc), 1), :
                ]

    for f in range(FIELDS):
        ext[f, pl.ds(8, nx), :] = pad[pl.ds(f * 128, 128), :].T

    to_left = pltpu.make_async_remote_copy(
        src_ref=ext.at[:, pl.ds(8, 8)],
        dst_ref=ext.at[:, pl.ds(8 + nx, 8)],
        send_sem=send_sem.at[8],
        recv_sem=recv_sem.at[8],
        device_id={"gx": left},
        device_id_type=MESH,
    )
    to_right = pltpu.make_async_remote_copy(
        src_ref=ext.at[:, pl.ds(nx, 8)],
        dst_ref=ext.at[:, pl.ds(0, 8)],
        send_sem=send_sem.at[9],
        recv_sem=recv_sem.at[9],
        device_id={"gx": right},
        device_id_type=MESH,
    )
    to_left.start()
    to_right.start()

    lane = lax.broadcasted_iota(jnp.int32, (8, 128), 1)
    slab = iz * nz - 1
    zglobal = jnp.zeros((8, 128), jnp.int32) + slab
    for j in range(1, nz + 3):
        zglobal = zglobal + (lane >= j * wide).astype(jnp.int32)
    height = (2 * zglobal + 1 - nz * gz).astype(jnp.float32) * (1.0 / (nz * gz))
    pull = -gravity * courant * height

    def up(values, axis):
        return pltpu.roll(values, 128 - (wide if axis == 0 else 1), 1)

    def down(values, axis):
        return pltpu.roll(values, wide if axis == 0 else 1, 1)

    def chunk(k):
        r = 7 + 8 * k
        now = [ext[f, pl.ds(r, 8), :] for f in range(FIELDS)]
        below = [ext[f, pl.ds(r - 1, 8), :] for f in range(7)]
        rho, vel, pre, faces = now[0], now[1:4], now[4], now[5:8]
        centre = [
            0.5 * (faces[0] + up(faces[0], 0)),
            0.5 * (faces[1] + up(faces[1], 1)),
            0.5 * (faces[2] + ext[FX, pl.ds(r + 1, 8), :]),
        ]
        cell = cell_terms(rho, vel, pre)
        fluxes = []
        for axis in range(3):
            if axis == 2:
                lrho, lvel, lpre = below[0], below[1:4], below[4]
                lmag = [
                    0.5 * (below[5] + up(below[5], 0)),
                    0.5 * (below[6] + up(below[6], 1)),
                    faces[2],
                ]
            else:
                lrho, lpre = down(rho, axis), down(pre, axis)
                lvel = [down(v, axis) for v in vel]
                lmag = [faces[c] if c == axis else down(centre[c], axis) for c in range(3)]
            umag = [faces[c] if c == axis else centre[c] for c in range(3)]
            lower = state_terms(cell_terms(lrho, lvel, lpre), lvel, lpre, lmag, axis)
            upper = state_terms(cell, vel, pre, umag, axis)
            fluxes.append(hll(lower, upper))
        squared = centre[0] * centre[0] + centre[1] * centre[1] + centre[2] * centre[2]
        base = [rho] + list(cell[4]) + [cell[3] + 0.5 * squared]
        fz, fy, fx = fluxes
        out = pl.ds(8 * k, 8)
        for m in range(5):
            change = up(fz[m], 0) - fz[m] + up(fy[m], 1) - fy[m]
            value = base[m] - courant * change
            if m == 1:
                value = value + rho * pull
            if m == 4:
                value = value + cell[4][0] * pull
            part[m, out, :] = value
            part[5 + m, out, :] = fx[m]
        part[10, out, :] = 0.25 * (fz[5] + down(fz[5], 1) - fy[5] - down(fy[5], 0))
        part[11, out, :] = fx[5] + down(fx[5], 0) - fz[6]
        part[12, out, :] = fz[6]
        part[13, out, :] = fy[6] - fx[6] - down(fx[6], 1)
        part[14, out, :] = fy[6]

    def body(k, carry):
        chunk(k)
        return carry

    count = nx // 8
    lax.fori_loop(1, count, body, 0)
    to_left.wait_recv()
    to_right.wait_recv()
    chunk(0)
    chunk(count)

    def finish(k, carry):
        at = 8 * k
        here, after, before = pl.ds(at + 1, 8), pl.ds(at + 2, 8), pl.ds(at, 8)
        for m in range(5):
            res[m, before, :] = part[m, here, :] - courant * (part[5 + m, after, :] - part[5 + m, here, :])
        ex = part[10, here, :]
        ey = 0.25 * (part[11, here, :] - part[12, before, :])
        ez = 0.25 * (part[13, here, :] + part[14, before, :])
        ey_next = 0.25 * (part[11, after, :] - part[12, here, :])
        ez_next = 0.25 * (part[13, after, :] + part[14, here, :])
        row = pl.ds(at + 8, 8)
        res[7, before, :] = ext[FX, row, :] - courant * ((up(ez, 1) - ez) - (up(ey, 0) - ey))
        res[6, before, :] = ext[FY, row, :] - courant * ((up(ex, 0) - ex) - (ez_next - ez))
        res[5, before, :] = ext[FZ, row, :] - courant * ((ey_next - ey) - (up(ex, 1) - ex))
        return carry

    lax.fori_loop(0, count, finish, 0)
    for m in range(8):
        pad[pl.ds(m * 128, 128), :] = res[m].T
        target, base = (cons_ref, m * plane) if m < 5 else (face_ref, (m - 5) * plane)
        for z in range(nz):
            target[pl.ds(base + z * ny, ny), :] = pad[pl.ds(m * 128 + (z + 1) * wide + 1, ny), :]

    for d in range(8):
        @pl.when(exists(*DIRS[d]))
        def _():
            message(d).wait_send()
    to_left.wait_send()
    to_right.wait_send()


def on_device(sizes, density, velocity, pressure, field, corona):
    nz, ny, nx = density.shape
    gz, gy, gx = sizes
    plane = nz * ny
    vmem = pl.BlockSpec(memory_space=pltpu.VMEM)
    f32 = jnp.float32
    rows = FIELDS * max(nz, ny) + max(nz, ny)
    conserved, faces = pl.pallas_call(
        functools.partial(kernel, (nz, ny, nx, gz, gy, gx)),
        out_shape=(
            jax.ShapeDtypeStruct((5 * plane, nx), f32),
            jax.ShapeDtypeStruct((3 * plane, nx), f32),
        ),
        in_specs=[vmem] * 4 + [pl.BlockSpec(memory_space=pltpu.SMEM)],
        out_specs=(vmem, vmem),
        scratch_shapes=[
            pltpu.VMEM((plane, nx), f32),
            pltpu.VMEM((8, rows, nx), f32),
            pltpu.VMEM((8, rows, nx), f32),
            pltpu.VMEM((FIELDS * 128, nx), f32),
            pltpu.VMEM((FIELDS, nx + 16, 128), f32),
            pltpu.VMEM((PARTS, nx + 8, 128), f32),
            pltpu.VMEM((8, nx, 128), f32),
            pltpu.SemaphoreType.DMA((10,)),
            pltpu.SemaphoreType.DMA((10,)),
        ],
        compiler_params=pltpu.CompilerParams(collective_id=0, has_side_effects=True),
    )(
        density.reshape(plane, nx),
        velocity.reshape(3 * plane, nx),
        pressure.reshape(plane, nx),
        field.reshape(3 * plane, nx),
        corona,
    )
    return conserved.reshape(5, nz, ny, nx), faces.reshape(3, nz, ny, nx)


def solution(mesh):
    sizes = tuple(mesh.shape[axis] for axis in ("gz", "gy", "gx"))
    return jax.shard_map(
        functools.partial(on_device, sizes),
        mesh=mesh,
        in_specs=(
            P("gz", "gy", "gx"),
            P(None, "gz", "gy", "gx"),
            P("gz", "gy", "gx"),
            P(None, "gz", "gy", "gx"),
            P(),
        ),
        out_specs=(P(None, "gz", "gy", "gx"), P(None, "gz", "gy", "gx")),
        check_vma=False,
    )
```

```python
import functools

import jax
import jax.numpy as jnp
from jax import lax
from jax.experimental import pallas as pl
from jax.experimental.pallas import tpu as pltpu
from jax.sharding import PartitionSpec as P

COOL_STEPS = 8
adiabatic = 5.0 / 3.0
courant = 0.08
cool_rate = 0.03
gravity = 1.0

MESH = pl.DeviceIdType.MESH
DIRS = ((0, -1), (0, 1), (-1, 0), (1, 0), (-1, -1), (-1, 1), (1, -1), (1, 1))
FIELDS = 8
FZ, FY, FX = 5, 6, 7
PARTS = 15


def fast_speed(sound, normal_sq, transverse_sq, inv_rho):
    along = normal_sq * inv_rho
    across = transverse_sq * inv_rho
    gap = sound - along - across
    return jnp.sqrt(0.5 * (sound + along + across + jnp.sqrt(gap * gap + 4.0 * sound * across)))


def state_terms(cell, velocity, pressure, magnetic, axis):
    rho, inv_rho, sound, hydro, momenta = cell
    others = [c for c in range(3) if c != axis]
    normal = magnetic[axis]
    normal_sq = normal * normal
    transverse_sq = magnetic[others[0]] * magnetic[others[0]] + magnetic[others[1]] * magnetic[others[1]]
    squared = transverse_sq + normal_sq
    half = 0.5 * squared
    total = pressure + half
    energy = hydro + half
    align = velocity[0] * magnetic[0] + velocity[1] * magnetic[1] + velocity[2] * magnetic[2]
    speed = fast_speed(sound, normal_sq, transverse_sq, inv_rho)
    va = velocity[axis]
    conserved = [rho] + list(momenta) + [energy] + [magnetic[c] for c in others]
    fluxes = [momenta[axis]]
    for c in range(3):
        moment = momenta[c] * va - magnetic[c] * normal
        if c == axis:
            moment = moment + total
        fluxes.append(moment)
    fluxes.append((energy + total) * va - normal * align)
    for c in others:
        fluxes.append(va * magnetic[c] - velocity[c] * normal)
    return va, speed, conserved, fluxes


def cell_terms(rho, velocity, pressure):
    inv_rho = 1.0 / rho
    momenta = [rho * v for v in velocity]
    kinetic = momenta[0] * velocity[0] + momenta[1] * velocity[1] + momenta[2] * velocity[2]
    hydro = pressure * (1.0 / (adiabatic - 1.0)) + 0.5 * kinetic
    return rho, inv_rho, adiabatic * pressure * inv_rho, hydro, momenta


def hll(lower, upper):
    slow = jnp.minimum(jnp.minimum(lower[0] - lower[1], upper[0] - upper[1]), 0.0)
    fast = jnp.maximum(jnp.maximum(lower[0] + lower[1], upper[0] + upper[1]), 0.0)
    inverse = 1.0 / (fast - slow)
    wl = fast * inverse
    wu = -slow * inverse
    wj = slow * wl
    return [
        wl * lower[3][m] + wu * upper[3][m] + wj * (upper[2][m] - lower[2][m]) for m in range(7)
    ]


def kernel(
    sizes, rho_hbm, vel_hbm, pre_hbm, fld_hbm, corona_hbm, res,
    stack, raw, marks, sbuf, rbuf, pad, ext, part, load_sem, send_sem, recv_sem,
):
    nz, ny, nx, gz, gy, gx = sizes
    plane = nz * ny
    wide = ny + 3
    iz, iy, ix = lax.axis_index("gz"), lax.axis_index("gy"), lax.axis_index("gx")
    left = lax.rem(ix + gx - 1, gx)
    right = lax.rem(ix + 1, gx)

    has_z = {-1: iz > 0, 0: None, 1: iz < gz - 1}
    has_y = {-1: iy > 0, 0: None, 1: iy < gy - 1}

    def exists(dz, dy):
        if dz == 0:
            return has_y[dy]
        if dy == 0:
            return has_z[dz]
        return jnp.logical_and(has_z[dz], has_y[dy])

    loads = [
        pltpu.make_async_copy(src, dst, load_sem.at[i])
        for i, (src, dst) in enumerate((
            (rho_hbm, stack.at[pl.ds(0, plane)]),
            (pre_hbm, raw),
            (corona_hbm, marks),
            (fld_hbm, stack.at[pl.ds(FZ * plane, 3 * plane)]),
            (vel_hbm, stack.at[pl.ds(plane, 3 * plane)]),
        ))
    ]
    for load in loads:
        load.start()

    barrier = pltpu.get_barrier_semaphore()
    for to in (left, right):
        pl.semaphore_signal(barrier, inc=1, device_id={"gx": to}, device_id_type=MESH)
    for dz, dy in DIRS:
        @pl.when(exists(dz, dy))
        def _():
            pl.semaphore_signal(
                barrier, inc=1, device_id={"gz": iz + dz, "gy": iy + dy}, device_id_type=MESH
            )

    for load in loads[:3]:
        load.wait()
    for z in range(nz):
        rows = pl.ds(z * ny, ny)
        rho = stack[rows, :]
        start = raw[rows, :]
        p = start
        for _ in range(COOL_STEPS):
            p = p / (1.0 + cool_rate * jnp.sqrt(rho * p))
        mark = jnp.full(p.shape, marks[iz * nz + z], jnp.int32)
        stack[pl.ds(4 * plane + z * ny, ny), :] = jnp.where(mark == 1, p, start)

    for load in loads[3:]:
        load.wait()

    def y_rows(f, y):
        return stack[pl.ds(f * plane + y, nz, stride=ny), :]

    def z_rows(f, z):
        return stack[pl.ds(f * plane + z * ny, ny), :]

    def one_row(f, z, y):
        return stack[pl.ds(f * plane + z * ny + y, 1), :]

    zf, yf = FIELDS * ny, FIELDS * nz
    for f in range(FIELDS):
        for d, at in ((0, 0), (1, ny - 1)):
            sbuf[d, pl.ds(f * nz, nz), :] = y_rows(f, at)
        for d, at in ((2, 0), (3, nz - 1)):
            sbuf[d, pl.ds(f * ny, ny), :] = z_rows(f, at)
        for d in range(4, 8):
            dz, dy = DIRS[d]
            sbuf[d, pl.ds(f, 1), :] = one_row(f, 0 if dz < 0 else nz - 1, 0 if dy < 0 else ny - 1)
    sbuf[0, pl.ds(yf, nz), :] = y_rows(FY, 1)
    sbuf[2, pl.ds(zf, ny), :] = z_rows(FZ, 1)
    sbuf[5, pl.ds(FIELDS, 1), :] = one_row(FZ, 1, ny - 1)
    sbuf[6, pl.ds(FIELDS, 1), :] = one_row(FY, nz - 1, 1)
    size = (yf + nz, yf, zf + ny, zf, 16, 16, 16, 16)

    for f in range(FIELDS):
        for z in range(nz):
            pad[pl.ds(f * 128 + (z + 1) * wide + 1, ny), :] = z_rows(f, z)

    pl.semaphore_wait(
        barrier,
        2 + sum(exists(dz, dy).astype(jnp.int32) for dz, dy in DIRS),
    )

    def message(d):
        dz, dy = DIRS[d]
        return pltpu.make_async_remote_copy(
            src_ref=sbuf.at[d, pl.ds(0, size[d])],
            dst_ref=rbuf.at[d, pl.ds(0, size[d])],
            send_sem=send_sem.at[d],
            recv_sem=recv_sem.at[d],
            device_id={"gz": iz + dz, "gy": iy + dy},
            device_id_type=MESH,
        )

    for d in (4, 5, 6, 7, 0, 1, 2, 3):
        @pl.when(exists(*DIRS[d]))
        def _():
            message(d).start()

    for d in range(4):
        dz, dy = DIRS[d]
        own = DIRS.index((-dz, -dy))
        step = nz if dz == 0 else ny

        @pl.when(jnp.logical_not(exists(-dz, -dy)))
        def _():
            for f in range(FIELDS):
                rbuf[d, pl.ds(f * step, step), :] = sbuf[own, pl.ds(f * step, step), :]
            if dz + dy < 0:
                f = FY if dz == 0 else FZ
                rbuf[d, pl.ds(FIELDS * step, step), :] = sbuf[own, pl.ds(f * step, step), :]

    for d in range(8):
        dz, dy = DIRS[d]

        @pl.when(exists(-dz, -dy))
        def _():
            message(d).wait_recv()

    for f in range(FIELDS):
        base = f * 128
        pad[pl.ds(base + wide, nz, stride=wide), :] = rbuf[1, pl.ds(f * nz, nz), :]
        pad[pl.ds(base + wide + ny + 1, nz, stride=wide), :] = rbuf[0, pl.ds(f * nz, nz), :]
        pad[pl.ds(base + 1, ny), :] = rbuf[3, pl.ds(f * ny, ny), :]
        pad[pl.ds(base + (nz + 1) * wide + 1, ny), :] = rbuf[2, pl.ds(f * ny, ny), :]
    pad[pl.ds(FY * 128 + wide + ny + 2, nz, stride=wide), :] = rbuf[0, pl.ds(yf, nz), :]
    pad[pl.ds(FZ * 128 + (nz + 2) * wide + 1, ny), :] = rbuf[2, pl.ds(zf, ny), :]

    def spot(z, y):
        return (z + 1) * wide + y + 1

    for d in range(4, 8):
        dz, dy = DIRS[d]
        zg, yg = (nz if dz < 0 else -1), (ny if dy < 0 else -1)
        zc, yc = min(max(zg, 0), nz - 1), min(max(yg, 0), ny - 1)
        both = exists(-dz, -dy)
        extra = {5: (FZ, 1, 0), 6: (FY, 0, 1)}.get(d)

        @pl.when(both)
        def _():
            pad[pl.ds(spot(zg, yg), FIELDS, stride=128), :] = rbuf[d, pl.ds(0, FIELDS), :]
            if extra:
                f, ez, ey = extra
                pad[pl.ds(f * 128 + spot(zg + ez, yg + ey), 1), :] = rbuf[d, pl.ds(FIELDS, 1), :]

        def copy_rows(zs, ys):
            pad[pl.ds(spot(zg, yg), FIELDS, stride=128), :] = pad[
                pl.ds(spot(zs, ys), FIELDS, stride=128), :
            ]

        @pl.when(jnp.logical_not(has_z[-dz]))
        def _():
            copy_rows(zc, yg)
            if extra:
                f, ez, ey = extra
                pad[pl.ds(f * 128 + spot(zg + ez, yg + ey), 1), :] = pad[
                    pl.ds(f * 128 + spot(zc, yg + ey), 1), :
                ]

        @pl.when(jnp.logical_and(has_z[-dz], jnp.logical_not(has_y[-dy])))
        def _():
            copy_rows(zg, yc)
            if extra:
                f, ez, ey = extra
                pad[pl.ds(f * 128 + spot(zg + ez, yg + ey), 1), :] = pad[
                    pl.ds(f * 128 + spot(zg + ez, yc), 1), :
                ]

    for f in range(FIELDS):
        ext[f, pl.ds(8, nx), :] = pad[pl.ds(f * 128, 128), :].T

    to_left = pltpu.make_async_remote_copy(
        src_ref=ext.at[:, pl.ds(8, 8)],
        dst_ref=ext.at[:, pl.ds(8 + nx, 8)],
        send_sem=send_sem.at[8],
        recv_sem=recv_sem.at[8],
        device_id={"gx": left},
        device_id_type=MESH,
    )
    to_right = pltpu.make_async_remote_copy(
        src_ref=ext.at[:, pl.ds(nx, 8)],
        dst_ref=ext.at[:, pl.ds(0, 8)],
        send_sem=send_sem.at[9],
        recv_sem=recv_sem.at[9],
        device_id={"gx": right},
        device_id_type=MESH,
    )
    to_left.start()
    to_right.start()

    lane = lax.broadcasted_iota(jnp.int32, (8, 128), 1)
    slab = iz * nz - 1
    zglobal = jnp.zeros((8, 128), jnp.int32) + slab
    for j in range(1, nz + 3):
        zglobal = zglobal + (lane >= j * wide).astype(jnp.int32)
    height = (2 * zglobal + 1 - nz * gz).astype(jnp.float32) * (1.0 / (nz * gz))
    pull = -gravity * courant * height

    def up(values, axis):
        return pltpu.roll(values, 128 - (wide if axis == 0 else 1), 1)

    def down(values, axis):
        return pltpu.roll(values, wide if axis == 0 else 1, 1)

    def chunk(k):
        r = 7 + 8 * k
        now = [ext[f, pl.ds(r, 8), :] for f in range(FIELDS)]
        below = [ext[f, pl.ds(r - 1, 8), :] for f in range(7)]
        rho, vel, pre, faces = now[0], now[1:4], now[4], now[5:8]
        centre = [
            0.5 * (faces[0] + up(faces[0], 0)),
            0.5 * (faces[1] + up(faces[1], 1)),
            0.5 * (faces[2] + ext[FX, pl.ds(r + 1, 8), :]),
        ]
        cell = cell_terms(rho, vel, pre)
        fluxes = []
        for axis in range(3):
            if axis == 2:
                lrho, lvel, lpre = below[0], below[1:4], below[4]
                lmag = [
                    0.5 * (below[5] + up(below[5], 0)),
                    0.5 * (below[6] + up(below[6], 1)),
                    faces[2],
                ]
            else:
                lrho, lpre = down(rho, axis), down(pre, axis)
                lvel = [down(v, axis) for v in vel]
                lmag = [faces[c] if c == axis else down(centre[c], axis) for c in range(3)]
            umag = [faces[c] if c == axis else centre[c] for c in range(3)]
            lower = state_terms(cell_terms(lrho, lvel, lpre), lvel, lpre, lmag, axis)
            upper = state_terms(cell, vel, pre, umag, axis)
            fluxes.append(hll(lower, upper))
        squared = centre[0] * centre[0] + centre[1] * centre[1] + centre[2] * centre[2]
        base = [rho] + list(cell[4]) + [cell[3] + 0.5 * squared]
        fz, fy, fx = fluxes
        out = pl.ds(8 * k, 8)
        for m in range(5):
            change = up(fz[m], 0) - fz[m] + up(fy[m], 1) - fy[m]
            value = base[m] - courant * change
            if m == 1:
                value = value + rho * pull
            if m == 4:
                value = value + cell[4][0] * pull
            part[m, out, :] = value
            part[5 + m, out, :] = fx[m]
        part[10, out, :] = 0.25 * (fz[5] + down(fz[5], 1) - fy[5] - down(fy[5], 0))
        part[11, out, :] = fx[5] + down(fx[5], 0) - fz[6]
        part[12, out, :] = fz[6]
        part[13, out, :] = fy[6] - fx[6] - down(fx[6], 1)
        part[14, out, :] = fy[6]

    def body(k, carry):
        chunk(k)
        return carry

    count = nx // 8
    lax.fori_loop(1, count, body, 0)
    to_left.wait_recv()
    to_right.wait_recv()
    chunk(0)
    chunk(count)

    def finish(k, carry):
        at = 8 * k
        here, after, before = pl.ds(at + 1, 8), pl.ds(at + 2, 8), pl.ds(at, 8)
        for m in range(5):
            res[m, before, :] = part[m, here, :] - courant * (part[5 + m, after, :] - part[5 + m, here, :])
        ex = part[10, here, :]
        ey = 0.25 * (part[11, here, :] - part[12, before, :])
        ez = 0.25 * (part[13, here, :] + part[14, before, :])
        ey_next = 0.25 * (part[11, after, :] - part[12, here, :])
        ez_next = 0.25 * (part[13, after, :] + part[14, here, :])
        row = pl.ds(at + 8, 8)
        res[7, before, :] = ext[FX, row, :] - courant * ((up(ez, 1) - ez) - (up(ey, 0) - ey))
        res[6, before, :] = ext[FY, row, :] - courant * ((up(ex, 0) - ex) - (ez_next - ez))
        res[5, before, :] = ext[FZ, row, :] - courant * ((ey_next - ey) - (up(ex, 1) - ex))
        return carry

    lax.fori_loop(0, count, finish, 0)
    for d in range(8):
        @pl.when(exists(*DIRS[d]))
        def _():
            message(d).wait_send()
    to_left.wait_send()
    to_right.wait_send()


def unpack_kernel(sizes, res, cons_ref, face_ref, turned, out, sem):
    nz, ny = sizes
    plane, wide = nz * ny, ny + 3
    copies = []
    for m in range(FIELDS):
        turned[m] = res[m].T
        for z in range(nz):
            out[pl.ds(m * plane + z * ny, ny), :] = turned[m, pl.ds((z + 1) * wide + 1, ny), :]
        target, base = (cons_ref, m * plane) if m < 5 else (face_ref, (m - 5) * plane)
        copies.append(pltpu.make_async_copy(
            out.at[pl.ds(m * plane, plane)], target.at[pl.ds(base, plane)], sem.at[m]
        ))
        copies[-1].start()
    for copy in copies:
        copy.wait()


def on_device(sizes, density, velocity, pressure, field, corona):
    nz, ny, nx = density.shape
    gz, gy, gx = sizes
    plane = nz * ny
    hbm = pl.BlockSpec(memory_space=pltpu.HBM)
    vmem = pl.BlockSpec(memory_space=pltpu.VMEM)
    f32 = jnp.float32
    rows = FIELDS * max(nz, ny) + max(nz, ny)
    result = pl.pallas_call(
        functools.partial(kernel, (nz, ny, nx, gz, gy, gx)),
        out_shape=pltpu.VMEM((FIELDS, nx, 128), f32),
        in_specs=[hbm] * 5,
        out_specs=vmem,
        scratch_shapes=[
            pltpu.VMEM((FIELDS * plane, nx), f32),
            pltpu.VMEM((plane, nx), f32),
            pltpu.SMEM(corona.shape, jnp.int32),
            pltpu.VMEM((8, rows, nx), f32),
            pltpu.VMEM((8, rows, nx), f32),
            pltpu.VMEM((FIELDS * 128, nx), f32),
            pltpu.VMEM((FIELDS, nx + 16, 128), f32),
            pltpu.VMEM((PARTS, nx + 8, 128), f32),
            pltpu.SemaphoreType.DMA((5,)),
            pltpu.SemaphoreType.DMA((10,)),
            pltpu.SemaphoreType.DMA((10,)),
        ],
        compiler_params=pltpu.CompilerParams(
            collective_id=0, has_side_effects=True, vmem_limit_bytes=16 << 20
        ),
    )(
        *(
            pltpu.with_memory_space_constraint(x, pltpu.HBM)
            for x in (
                density.reshape(plane, nx),
                velocity.reshape(3 * plane, nx),
                pressure.reshape(plane, nx),
                field.reshape(3 * plane, nx),
                corona,
            )
        )
    )
    conserved, faces = pl.pallas_call(
        functools.partial(unpack_kernel, (nz, ny)),
        out_shape=(
            jax.ShapeDtypeStruct((5 * plane, nx), f32),
            jax.ShapeDtypeStruct((3 * plane, nx), f32),
        ),
        in_specs=[vmem],
        out_specs=(hbm, hbm),
        scratch_shapes=[
            pltpu.VMEM((FIELDS, 128, nx), f32),
            pltpu.VMEM((FIELDS * plane, nx), f32),
            pltpu.SemaphoreType.DMA((FIELDS,)),
        ],
        compiler_params=pltpu.CompilerParams(vmem_limit_bytes=16 << 20),
    )(result)
    return conserved.reshape(5, nz, ny, nx), faces.reshape(3, nz, ny, nx)


def solution(mesh):
    sizes = tuple(mesh.shape[axis] for axis in ("gz", "gy", "gx"))
    return jax.shard_map(
        functools.partial(on_device, sizes),
        mesh=mesh,
        in_specs=(
            P("gz", "gy", "gx"),
            P(None, "gz", "gy", "gx"),
            P("gz", "gy", "gx"),
            P(None, "gz", "gy", "gx"),
            P(),
        ),
        out_specs=(P(None, "gz", "gy", "gx"), P(None, "gz", "gy", "gx")),
        check_vma=False,
    )
```

```python
import functools

import jax
import jax.numpy as jnp
from jax import lax
from jax.experimental import pallas as pl
from jax.experimental.pallas import tpu as pltpu
from jax.sharding import PartitionSpec as P

COOL_STEPS = 8
adiabatic = 5.0 / 3.0
courant = 0.08
cool_rate = 0.03
gravity = 1.0

MESH = pl.DeviceIdType.MESH
DIRS = ((0, -1), (0, 1), (-1, 0), (1, 0), (-1, -1), (-1, 1), (1, -1), (1, 1))
FIELDS = 8
FZ, FY, FX = 5, 6, 7
PARTS = 15
TINY = 1e-36


def root(values):
    return values * lax.rsqrt(values)


def fast_speed(half_sound, squared, transverse_sq, half_inverse):
    both = squared * half_inverse
    gap = half_sound - both
    inner = gap * gap + (4.0 * half_sound) * (transverse_sq * half_inverse)
    return root(half_sound + both + root(jnp.maximum(inner, TINY)))


def state_terms(cell, velocity, pressure, magnetic, axis):
    rho, half_inverse, half_sound, hydro, momenta = cell
    others = [c for c in range(3) if c != axis]
    normal = magnetic[axis]
    normal_sq = normal * normal
    transverse_sq = magnetic[others[0]] * magnetic[others[0]] + magnetic[others[1]] * magnetic[others[1]]
    squared = transverse_sq + normal_sq
    half = 0.5 * squared
    total = pressure + half
    energy = hydro + half
    align = velocity[0] * magnetic[0] + velocity[1] * magnetic[1] + velocity[2] * magnetic[2]
    speed = fast_speed(half_sound, squared, transverse_sq, half_inverse)
    va = velocity[axis]
    conserved = [rho] + list(momenta) + [energy] + [magnetic[c] for c in others]
    fluxes = [momenta[axis]]
    for c in range(3):
        moment = momenta[c] * va - magnetic[c] * normal
        if c == axis:
            moment = moment + total
        fluxes.append(moment)
    fluxes.append((energy + total) * va - normal * align)
    for c in others:
        fluxes.append(va * magnetic[c] - velocity[c] * normal)
    return va, speed, conserved, fluxes


def cell_terms(rho, velocity, pressure):
    half_inverse = 0.5 / rho
    momenta = [rho * v for v in velocity]
    kinetic = momenta[0] * velocity[0] + momenta[1] * velocity[1] + momenta[2] * velocity[2]
    hydro = pressure * (1.0 / (adiabatic - 1.0)) + 0.5 * kinetic
    return rho, half_inverse, adiabatic * pressure * half_inverse, hydro, momenta


def hll(lower, upper):
    slow = jnp.minimum(jnp.minimum(lower[0] - lower[1], upper[0] - upper[1]), 0.0)
    fast = jnp.maximum(jnp.maximum(lower[0] + lower[1], upper[0] + upper[1]), 0.0)
    inverse = 1.0 / (fast - slow)
    wl = fast * inverse
    wu = -slow * inverse
    wj = slow * wl
    return [
        wl * lower[3][m] + wu * upper[3][m] + wj * (upper[2][m] - lower[2][m]) for m in range(7)
    ]


def kernel(
    sizes, rho_hbm, vel_hbm, pre_hbm, fld_hbm, corona_hbm, res,
    stack, raw, marks, sbuf, rbuf, pad, ext, xsend, xrecv, part, load_sem, send_sem, recv_sem, ready,
):
    nz, ny, nx, gz, gy, gx = sizes
    plane = nz * ny
    wide = ny + 3
    tall = nx + 16
    iz, iy, ix = lax.axis_index("gz"), lax.axis_index("gy"), lax.axis_index("gx")
    left = lax.rem(ix + gx - 1, gx)
    right = lax.rem(ix + 1, gx)

    has_z = {-1: iz > 0, 0: None, 1: iz < gz - 1}
    has_y = {-1: iy > 0, 0: None, 1: iy < gy - 1}

    def exists(dz, dy):
        if dz == 0:
            return has_y[dy]
        if dy == 0:
            return has_z[dz]
        return jnp.logical_and(has_z[dz], has_y[dy])

    loads = [
        pltpu.make_async_copy(src, dst, load_sem.at[i])
        for i, (src, dst) in enumerate((
            (rho_hbm, stack.at[pl.ds(0, plane)]),
            (pre_hbm, raw),
            (corona_hbm, marks),
            (fld_hbm, stack.at[pl.ds(FZ * plane, 3 * plane)]),
            (vel_hbm, stack.at[pl.ds(plane, 3 * plane)]),
        ))
    ]
    for load in loads:
        load.start()

    barrier = pltpu.get_barrier_semaphore()
    for to in (left, right):
        pl.semaphore_signal(barrier, inc=1, device_id={"gx": to}, device_id_type=MESH)
    for dz, dy in DIRS[:4]:
        @pl.when(exists(dz, dy))
        def _():
            pl.semaphore_signal(
                barrier, inc=1, device_id={"gz": iz + dz, "gy": iy + dy}, device_id_type=MESH
            )

    for load in loads[:3]:
        load.wait()
    for z in range(nz):
        rows = pl.ds(z * ny, ny)
        rho = stack[rows, :]
        start = raw[rows, :]
        p = start
        for _ in range(COOL_STEPS):
            p = p / (1.0 + cool_rate * jnp.sqrt(rho * p))
        mark = jnp.full(p.shape, marks[iz * nz + z], jnp.int32)
        stack[pl.ds(4 * plane + z * ny, ny), :] = jnp.where(mark == 1, p, start)

    for load in loads[3:]:
        load.wait()

    def y_rows(f, y):
        return stack[pl.ds(f * plane + y, nz, stride=ny), :]

    def z_rows(f, z):
        return stack[pl.ds(f * plane + z * ny, ny), :]

    def one_row(f, z, y):
        return stack[pl.ds(f * plane + z * ny + y, 1), :]

    zf, yf = FIELDS * ny, FIELDS * nz
    for f in range(FIELDS):
        for d, at in ((0, 0), (1, ny - 1)):
            sbuf[d, pl.ds(f * nz, nz), :] = y_rows(f, at)
        for d, at in ((2, 0), (3, nz - 1)):
            sbuf[d, pl.ds(f * ny, ny), :] = z_rows(f, at)
        for d in range(4, 8):
            dz, dy = DIRS[d]
            sbuf[d, pl.ds(f, 1), :] = one_row(f, 0 if dz < 0 else nz - 1, 0 if dy < 0 else ny - 1)
    sbuf[0, pl.ds(yf, nz), :] = y_rows(FY, 1)
    sbuf[2, pl.ds(zf, ny), :] = z_rows(FZ, 1)
    sbuf[5, pl.ds(FIELDS, 1), :] = one_row(FZ, 1, ny - 1)
    sbuf[6, pl.ds(FIELDS, 1), :] = one_row(FY, nz - 1, 1)
    size = (yf + nz, yf, zf + ny, zf, 16, 16, 16, 16)

    for f in range(FIELDS):
        for z in range(nz):
            pad[pl.ds(f * 128 + (z + 1) * wide + 1, ny), :] = z_rows(f, z)

    for d in range(4):
        dz, dy = DIRS[d]
        own = DIRS.index((-dz, -dy))
        step = nz if dz == 0 else ny

        @pl.when(jnp.logical_not(exists(-dz, -dy)))
        def _():
            for f in range(FIELDS):
                rbuf[d, pl.ds(f * step, step), :] = sbuf[own, pl.ds(f * step, step), :]
            if dz + dy < 0:
                f = FY if dz == 0 else FZ
                rbuf[d, pl.ds(FIELDS * step, step), :] = sbuf[own, pl.ds(f * step, step), :]

    pl.semaphore_wait(
        barrier,
        2 + sum(exists(dz, dy).astype(jnp.int32) for dz, dy in DIRS[:4]),
    )

    for dz in (-1, 1):
        @pl.when(has_z[dz])
        def _():
            pl.semaphore_signal(ready, inc=1, device_id={"gz": iz + dz}, device_id_type=MESH)

    def message(d):
        dz, dy = DIRS[d]
        return pltpu.make_async_remote_copy(
            src_ref=sbuf.at[d, pl.ds(0, size[d])],
            dst_ref=rbuf.at[d, pl.ds(0, size[d])],
            send_sem=send_sem.at[d],
            recv_sem=recv_sem.at[d],
            device_id={"gz": iz + dz, "gy": iy + dy},
            device_id_type=MESH,
        )

    for d in range(8):
        if d == 4:
            pl.semaphore_wait(ready, has_z[-1].astype(jnp.int32) + has_z[1].astype(jnp.int32))

        @pl.when(exists(*DIRS[d]))
        def _():
            message(d).start()

    for d in range(8):
        dz, dy = DIRS[d]

        @pl.when(exists(-dz, -dy))
        def _():
            message(d).wait_recv()

    for f in range(FIELDS):
        base = f * 128
        pad[pl.ds(base + wide, nz, stride=wide), :] = rbuf[1, pl.ds(f * nz, nz), :]
        pad[pl.ds(base + wide + ny + 1, nz, stride=wide), :] = rbuf[0, pl.ds(f * nz, nz), :]
        pad[pl.ds(base + 1, ny), :] = rbuf[3, pl.ds(f * ny, ny), :]
        pad[pl.ds(base + (nz + 1) * wide + 1, ny), :] = rbuf[2, pl.ds(f * ny, ny), :]
    pad[pl.ds(FY * 128 + wide + ny + 2, nz, stride=wide), :] = rbuf[0, pl.ds(yf, nz), :]
    pad[pl.ds(FZ * 128 + (nz + 2) * wide + 1, ny), :] = rbuf[2, pl.ds(zf, ny), :]

    def spot(z, y):
        return (z + 1) * wide + y + 1

    for d in range(4, 8):
        dz, dy = DIRS[d]
        zg, yg = (nz if dz < 0 else -1), (ny if dy < 0 else -1)
        zc, yc = min(max(zg, 0), nz - 1), min(max(yg, 0), ny - 1)
        both = exists(-dz, -dy)
        extra = {5: (FZ, 1, 0), 6: (FY, 0, 1)}.get(d)

        @pl.when(both)
        def _():
            pad[pl.ds(spot(zg, yg), FIELDS, stride=128), :] = rbuf[d, pl.ds(0, FIELDS), :]
            if extra:
                f, ez, ey = extra
                pad[pl.ds(f * 128 + spot(zg + ez, yg + ey), 1), :] = rbuf[d, pl.ds(FIELDS, 1), :]

        def copy_rows(zs, ys):
            pad[pl.ds(spot(zg, yg), FIELDS, stride=128), :] = pad[
                pl.ds(spot(zs, ys), FIELDS, stride=128), :
            ]

        @pl.when(jnp.logical_not(has_z[-dz]))
        def _():
            copy_rows(zc, yg)
            if extra:
                f, ez, ey = extra
                pad[pl.ds(f * 128 + spot(zg + ez, yg + ey), 1), :] = pad[
                    pl.ds(f * 128 + spot(zc, yg + ey), 1), :
                ]

        @pl.when(jnp.logical_and(has_z[-dz], jnp.logical_not(has_y[-dy])))
        def _():
            copy_rows(zg, yc)
            if extra:
                f, ez, ey = extra
                pad[pl.ds(f * 128 + spot(zg + ez, yg + ey), 1), :] = pad[
                    pl.ds(f * 128 + spot(zg + ez, yc), 1), :
                ]

    for f in range(FIELDS):
        ext[pl.ds(f * tall + 8, nx), :] = pad[pl.ds(f * 128, 128), :].T
    xsend[pl.ds(0, FIELDS), :] = ext[pl.ds(8, FIELDS, stride=tall), :]
    xsend[pl.ds(FIELDS, 1), :] = ext[pl.ds(FX * tall + 9, 1), :]
    xsend[pl.ds(16, FIELDS), :] = ext[pl.ds(7 + nx, FIELDS, stride=tall), :]

    to_left = pltpu.make_async_remote_copy(
        src_ref=xsend.at[pl.ds(0, 16)],
        dst_ref=xrecv.at[pl.ds(0, 16)],
        send_sem=send_sem.at[8],
        recv_sem=recv_sem.at[8],
        device_id={"gx": left},
        device_id_type=MESH,
    )
    to_right = pltpu.make_async_remote_copy(
        src_ref=xsend.at[pl.ds(16, 8)],
        dst_ref=xrecv.at[pl.ds(16, 8)],
        send_sem=send_sem.at[9],
        recv_sem=recv_sem.at[9],
        device_id={"gx": right},
        device_id_type=MESH,
    )
    lane = lax.broadcasted_iota(jnp.int32, (8, 128), 1)
    slab = iz * nz - 1
    zglobal = jnp.zeros((8, 128), jnp.int32) + slab
    for j in range(1, nz + 3):
        zglobal = zglobal + (lane >= j * wide).astype(jnp.int32)
    height = (2 * zglobal + 1 - nz * gz).astype(jnp.float32) * (1.0 / (nz * gz))
    pull = -gravity * courant * height
    to_left.start()
    to_right.start()

    def up(values, axis):
        return pltpu.roll(values, 128 - (wide if axis == 0 else 1), 1)

    def down(values, axis):
        return pltpu.roll(values, wide if axis == 0 else 1, 1)

    def chunk(k):
        r = 7 + 8 * k
        now = [ext[pl.ds(f * tall + r, 8), :] for f in range(FIELDS)]
        below = [ext[pl.ds(f * tall + r - 1, 8), :] for f in range(7)]
        rho, vel, pre, faces = now[0], now[1:4], now[4], now[5:8]
        centre = [
            0.5 * (faces[0] + up(faces[0], 0)),
            0.5 * (faces[1] + up(faces[1], 1)),
            0.5 * (faces[2] + ext[pl.ds(FX * tall + r + 1, 8), :]),
        ]
        cell = cell_terms(rho, vel, pre)
        fluxes = []
        for axis in range(3):
            if axis == 2:
                lrho, lvel, lpre = below[0], below[1:4], below[4]
                lcell = cell_terms(lrho, lvel, lpre)
                lmag = [
                    0.5 * (below[5] + up(below[5], 0)),
                    0.5 * (below[6] + up(below[6], 1)),
                    faces[2],
                ]
            else:
                lrho, lpre = down(rho, axis), down(pre, axis)
                lvel = [down(v, axis) for v in vel]
                lcell = (
                    lrho, down(cell[1], axis), down(cell[2], axis), down(cell[3], axis),
                    [lrho * v for v in lvel],
                )
                lmag = [faces[c] if c == axis else down(centre[c], axis) for c in range(3)]
            umag = [faces[c] if c == axis else centre[c] for c in range(3)]
            lower = state_terms(lcell, lvel, lpre, lmag, axis)
            upper = state_terms(cell, vel, pre, umag, axis)
            fluxes.append(hll(lower, upper))
        squared = centre[0] * centre[0] + centre[1] * centre[1] + centre[2] * centre[2]
        base = [rho] + list(cell[4]) + [cell[3] + 0.5 * squared]
        fz, fy, fx = fluxes
        out = pl.ds(8 * k, 8)
        for m in range(5):
            change = up(fz[m], 0) - fz[m] + up(fy[m], 1) - fy[m]
            value = base[m] - courant * change
            if m == 1:
                value = value + rho * pull
            if m == 4:
                value = value + cell[4][0] * pull
            part[m, out, :] = value
            part[5 + m, out, :] = fx[m]
        part[10, out, :] = 0.25 * (fz[5] + down(fz[5], 1) - fy[5] - down(fy[5], 0))
        part[11, out, :] = fx[5] + down(fx[5], 0) - fz[6]
        part[12, out, :] = fz[6]
        part[13, out, :] = fy[6] - fx[6] - down(fx[6], 1)
        part[14, out, :] = fy[6]

    count = nx // 8
    for k in range(1, count):
        chunk(k)
    to_left.wait_recv()
    to_right.wait_recv()
    ext[pl.ds(8 + nx, FIELDS, stride=tall), :] = xrecv[pl.ds(0, FIELDS), :]
    ext[pl.ds(FX * tall + 9 + nx, 1), :] = xrecv[pl.ds(FIELDS, 1), :]
    ext[pl.ds(7, FIELDS, stride=tall), :] = xrecv[pl.ds(16, FIELDS), :]
    chunk(0)
    chunk(count)

    def finish(k):
        at = 8 * k
        here, after, before = pl.ds(at + 1, 8), pl.ds(at + 2, 8), pl.ds(at, 8)
        for m in range(5):
            res[m, before, :] = part[m, here, :] - courant * (part[5 + m, after, :] - part[5 + m, here, :])
        ex = part[10, here, :]
        ey = 0.25 * (part[11, here, :] - part[12, before, :])
        ez = 0.25 * (part[13, here, :] + part[14, before, :])
        ey_next = 0.25 * (part[11, after, :] - part[12, here, :])
        ez_next = 0.25 * (part[13, after, :] + part[14, here, :])
        res[7, before, :] = ext[pl.ds(FX * tall + at + 8, 8), :] - courant * ((up(ez, 1) - ez) - (up(ey, 0) - ey))
        res[6, before, :] = ext[pl.ds(FY * tall + at + 8, 8), :] - courant * ((up(ex, 0) - ex) - (ez_next - ez))
        res[5, before, :] = ext[pl.ds(FZ * tall + at + 8, 8), :] - courant * ((ey_next - ey) - (up(ex, 1) - ex))

    for k in range(count):
        finish(k)
    for d in range(8):
        @pl.when(exists(*DIRS[d]))
        def _():
            message(d).wait_send()
    to_left.wait_send()
    to_right.wait_send()


def unpack_kernel(sizes, res, cons_ref, face_ref, turned, out, sem):
    nz, ny = sizes
    plane, wide = nz * ny, ny + 3
    copies = []
    for m in range(FIELDS):
        turned[m] = res[m].T
        for z in range(nz):
            out[pl.ds(m * plane + z * ny, ny), :] = turned[m, pl.ds((z + 1) * wide + 1, ny), :]
        target, base = (cons_ref, m * plane) if m < 5 else (face_ref, (m - 5) * plane)
        copies.append(pltpu.make_async_copy(
            out.at[pl.ds(m * plane, plane)], target.at[pl.ds(base, plane)], sem.at[m]
        ))
        copies[-1].start()
    for copy in copies:
        copy.wait()


def on_device(sizes, density, velocity, pressure, field, corona):
    nz, ny, nx = density.shape
    gz, gy, gx = sizes
    plane = nz * ny
    hbm = pl.BlockSpec(memory_space=pltpu.HBM)
    vmem = pl.BlockSpec(memory_space=pltpu.VMEM)
    f32 = jnp.float32
    rows = FIELDS * max(nz, ny) + max(nz, ny)
    result = pl.pallas_call(
        functools.partial(kernel, (nz, ny, nx, gz, gy, gx)),
        out_shape=pltpu.VMEM((FIELDS, nx, 128), f32),
        in_specs=[hbm] * 5,
        out_specs=vmem,
        scratch_shapes=[
            pltpu.VMEM((FIELDS * plane, nx), f32),
            pltpu.VMEM((plane, nx), f32),
            pltpu.SMEM(corona.shape, jnp.int32),
            pltpu.VMEM((8, rows, nx), f32),
            pltpu.VMEM((8, rows, nx), f32),
            pltpu.VMEM((FIELDS * 128, nx), f32),
            pltpu.VMEM((FIELDS * (nx + 16), 128), f32),
            pltpu.VMEM((24, 128), f32),
            pltpu.VMEM((24, 128), f32),
            pltpu.VMEM((PARTS, nx + 8, 128), f32),
            pltpu.SemaphoreType.DMA((5,)),
            pltpu.SemaphoreType.DMA((10,)),
            pltpu.SemaphoreType.DMA((10,)),
            pltpu.SemaphoreType.REGULAR,
        ],
        compiler_params=pltpu.CompilerParams(
            collective_id=0, has_side_effects=True, vmem_limit_bytes=16 << 20
        ),
    )(
        *(
            pltpu.with_memory_space_constraint(x, pltpu.HBM)
            for x in (
                density.reshape(plane, nx),
                velocity.reshape(3 * plane, nx),
                pressure.reshape(plane, nx),
                field.reshape(3 * plane, nx),
                corona,
            )
        )
    )
    conserved, faces = pl.pallas_call(
        functools.partial(unpack_kernel, (nz, ny)),
        out_shape=(
            jax.ShapeDtypeStruct((5 * plane, nx), f32),
            jax.ShapeDtypeStruct((3 * plane, nx), f32),
        ),
        in_specs=[vmem],
        out_specs=(hbm, hbm),
        scratch_shapes=[
            pltpu.VMEM((FIELDS, 128, nx), f32),
            pltpu.VMEM((FIELDS * plane, nx), f32),
            pltpu.SemaphoreType.DMA((FIELDS,)),
        ],
        compiler_params=pltpu.CompilerParams(vmem_limit_bytes=16 << 20),
    )(result)
    return conserved.reshape(5, nz, ny, nx), faces.reshape(3, nz, ny, nx)


def solution(mesh):
    sizes = tuple(mesh.shape[axis] for axis in ("gz", "gy", "gx"))
    return jax.shard_map(
        functools.partial(on_device, sizes),
        mesh=mesh,
        in_specs=(
            P("gz", "gy", "gx"),
            P(None, "gz", "gy", "gx"),
            P("gz", "gy", "gx"),
            P(None, "gz", "gy", "gx"),
            P(),
        ),
        out_specs=(P(None, "gz", "gy", "gx"), P(None, "gz", "gy", "gx")),
        check_vma=False,
    )
```

```python
import functools

import jax
import jax.numpy as jnp
from jax import lax
from jax.experimental import pallas as pl
from jax.experimental.pallas import tpu as pltpu
from jax.sharding import PartitionSpec as P

COOL_STEPS = 8
adiabatic = 5.0 / 3.0
courant = 0.08
cool_rate = 0.03
gravity = 1.0

MESH = pl.DeviceIdType.MESH
DIRS = ((0, -1), (0, 1), (-1, 0), (1, 0), (-1, -1), (-1, 1), (1, -1), (1, 1))
FIELDS = 8
FZ, FY, FX = 5, 6, 7
PARTS = 15
TINY = 1e-36


def root(values):
    return values * lax.rsqrt(values)


def fast_speed(half_sound, half_squared, transverse_sq, half_inverse):
    both = half_squared * (2.0 * half_inverse)
    gap = half_sound - both
    inner = gap * gap + (4.0 * half_sound) * (transverse_sq * half_inverse)
    return root(half_sound + both + root(jnp.maximum(inner, TINY)))


def state_terms(cell, velocity, pressure, magnetic, axis):
    rho, half_inverse, half_sound, hydro, momenta = cell
    one, two = [c for c in range(3) if c != axis]
    normal = magnetic[axis]
    normal_sq = normal * normal
    transverse_sq = magnetic[one] * magnetic[one] + magnetic[two] * magnetic[two]
    half = 0.5 * (transverse_sq + normal_sq)
    energy = hydro + half
    tension = pressure + half - normal_sq
    align = velocity[one] * magnetic[one] + velocity[two] * magnetic[two]
    speed = fast_speed(half_sound, half, transverse_sq, half_inverse)
    va = velocity[axis]
    conserved = [rho] + list(momenta) + [energy]
    work = tension * va - normal * align
    return va, speed, conserved, tension, work, velocity, magnetic


def cell_terms(rho, velocity, pressure):
    half_inverse = 0.5 / rho
    momenta = [rho * v for v in velocity]
    kinetic = momenta[0] * velocity[0] + momenta[1] * velocity[1] + momenta[2] * velocity[2]
    hydro = pressure * (1.0 / (adiabatic - 1.0)) + 0.5 * kinetic
    return rho, half_inverse, adiabatic * pressure * half_inverse, hydro, momenta


def hll(lower, upper, axis):
    low, high = lower[0] - lower[1], lower[0] + lower[1]
    slow = jnp.minimum(jnp.minimum(low, upper[0] - upper[1]), 0.0)
    fast = jnp.maximum(jnp.maximum(high, upper[0] + upper[1]), 0.0)
    inverse = 1.0 / (fast - slow)
    wl = fast * inverse
    wu = -slow * inverse
    wj = slow * wl
    al = wl * lower[0] - wj
    au = wu * upper[0] + wj
    normal = upper[6][axis]
    bl, bu = wl * normal, wu * normal

    def carried(one, two):
        return al * one + au * two

    others = [c for c in range(3) if c != axis]
    result = [carried(lower[2][0], upper[2][0])]
    for c in range(3):
        value = carried(lower[2][1 + c], upper[2][1 + c])
        if c == axis:
            value = value + (wl * lower[3] + wu * upper[3])
        else:
            value = value - (bl * lower[6][c] + bu * upper[6][c])
        result.append(value)
    result.append(carried(lower[2][4], upper[2][4]) + (wl * lower[4] + wu * upper[4]))
    for c in others:
        result.append(
            carried(lower[6][c], upper[6][c]) - (bl * lower[5][c] + bu * upper[5][c])
        )
    return result


def kernel(
    sizes, rho_hbm, vel_hbm, pre_hbm, fld_hbm, corona_hbm, res,
    stack, raw, marks, sbuf, rbuf, pad, ext, xsend, xrecv, part, load_sem, send_sem, recv_sem,
):
    nz, ny, nx, gz, gy, gx = sizes
    plane = nz * ny
    wide = ny + 3
    tall = nx + 16
    iz, iy, ix = lax.axis_index("gz"), lax.axis_index("gy"), lax.axis_index("gx")
    left = lax.rem(ix + gx - 1, gx)
    right = lax.rem(ix + 1, gx)

    has_z = {-1: iz > 0, 0: None, 1: iz < gz - 1}
    has_y = {-1: iy > 0, 0: None, 1: iy < gy - 1}

    def exists(dz, dy):
        if dz == 0:
            return has_y[dy]
        if dy == 0:
            return has_z[dz]
        return jnp.logical_and(has_z[dz], has_y[dy])

    loads = [
        pltpu.make_async_copy(src, dst, load_sem.at[i])
        for i, (src, dst) in enumerate((
            (rho_hbm, stack.at[pl.ds(0, plane)]),
            (pre_hbm, raw),
            (corona_hbm, marks),
            (fld_hbm, stack.at[pl.ds(FZ * plane, 3 * plane)]),
            (vel_hbm, stack.at[pl.ds(plane, 3 * plane)]),
        ))
    ]
    for load in loads:
        load.start()

    barrier = pltpu.get_barrier_semaphore()
    for to in (left, right):
        pl.semaphore_signal(barrier, inc=1, device_id={"gx": to}, device_id_type=MESH)
    for dz, dy in DIRS:
        @pl.when(exists(dz, dy))
        def _():
            pl.semaphore_signal(
                barrier, inc=1, device_id={"gz": iz + dz, "gy": iy + dy}, device_id_type=MESH
            )

    for load in loads[:3]:
        load.wait()
    for z in range(nz):
        rows = pl.ds(z * ny, ny)
        rho = stack[rows, :]
        start = raw[rows, :]
        p = start
        for _ in range(COOL_STEPS):
            p = p / (1.0 + cool_rate * jnp.sqrt(rho * p))
        mark = jnp.full(p.shape, marks[iz * nz + z], jnp.int32)
        stack[pl.ds(4 * plane + z * ny, ny), :] = jnp.where(mark == 1, p, start)

    for load in loads[3:]:
        load.wait()

    def y_rows(f, y):
        return stack[pl.ds(f * plane + y, nz, stride=ny), :]

    def z_rows(f, z):
        return stack[pl.ds(f * plane + z * ny, ny), :]

    def one_row(f, z, y):
        return stack[pl.ds(f * plane + z * ny + y, 1), :]

    zf, yf = FIELDS * ny, FIELDS * nz
    for f in range(FIELDS):
        for d, at in ((0, 0), (1, ny - 1)):
            sbuf[d, pl.ds(f * nz, nz), :] = y_rows(f, at)
        for d, at in ((2, 0), (3, nz - 1)):
            sbuf[d, pl.ds(f * ny, ny), :] = z_rows(f, at)
        for d in range(4, 8):
            dz, dy = DIRS[d]
            sbuf[d, pl.ds(f, 1), :] = one_row(f, 0 if dz < 0 else nz - 1, 0 if dy < 0 else ny - 1)
    sbuf[0, pl.ds(yf, nz), :] = y_rows(FY, 1)
    sbuf[2, pl.ds(zf, ny), :] = z_rows(FZ, 1)
    sbuf[5, pl.ds(FIELDS, 1), :] = one_row(FZ, 1, ny - 1)
    sbuf[6, pl.ds(FIELDS, 1), :] = one_row(FY, nz - 1, 1)
    size = (yf + nz, yf, zf + ny, zf, 16, 16, 16, 16)

    for f in range(FIELDS):
        for z in range(nz):
            pad[pl.ds(f * 128 + (z + 1) * wide + 1, ny), :] = z_rows(f, z)

    for d in range(4):
        dz, dy = DIRS[d]
        own = DIRS.index((-dz, -dy))
        step = nz if dz == 0 else ny

        @pl.when(jnp.logical_not(exists(-dz, -dy)))
        def _():
            for f in range(FIELDS):
                rbuf[d, pl.ds(f * step, step), :] = sbuf[own, pl.ds(f * step, step), :]
            if dz + dy < 0:
                f = FY if dz == 0 else FZ
                rbuf[d, pl.ds(FIELDS * step, step), :] = sbuf[own, pl.ds(f * step, step), :]

    pl.semaphore_wait(
        barrier,
        2 + sum(exists(dz, dy).astype(jnp.int32) for dz, dy in DIRS),
    )

    def message(d):
        dz, dy = DIRS[d]
        return pltpu.make_async_remote_copy(
            src_ref=sbuf.at[d, pl.ds(0, size[d])],
            dst_ref=rbuf.at[d, pl.ds(0, size[d])],
            send_sem=send_sem.at[d],
            recv_sem=recv_sem.at[d],
            device_id={"gz": iz + dz, "gy": iy + dy},
            device_id_type=MESH,
        )

    for d in range(8):
        @pl.when(exists(*DIRS[d]))
        def _():
            message(d).start()

    for d in range(8):
        dz, dy = DIRS[d]

        @pl.when(exists(-dz, -dy))
        def _():
            message(d).wait_recv()

    for f in range(FIELDS):
        base = f * 128
        pad[pl.ds(base + wide, nz, stride=wide), :] = rbuf[1, pl.ds(f * nz, nz), :]
        pad[pl.ds(base + wide + ny + 1, nz, stride=wide), :] = rbuf[0, pl.ds(f * nz, nz), :]
        pad[pl.ds(base + 1, ny), :] = rbuf[3, pl.ds(f * ny, ny), :]
        pad[pl.ds(base + (nz + 1) * wide + 1, ny), :] = rbuf[2, pl.ds(f * ny, ny), :]
    pad[pl.ds(FY * 128 + wide + ny + 2, nz, stride=wide), :] = rbuf[0, pl.ds(yf, nz), :]
    pad[pl.ds(FZ * 128 + (nz + 2) * wide + 1, ny), :] = rbuf[2, pl.ds(zf, ny), :]

    def spot(z, y):
        return (z + 1) * wide + y + 1

    for d in range(4, 8):
        dz, dy = DIRS[d]
        zg, yg = (nz if dz < 0 else -1), (ny if dy < 0 else -1)
        zc, yc = min(max(zg, 0), nz - 1), min(max(yg, 0), ny - 1)
        both = exists(-dz, -dy)
        extra = {5: (FZ, 1, 0), 6: (FY, 0, 1)}.get(d)

        @pl.when(both)
        def _():
            pad[pl.ds(spot(zg, yg), FIELDS, stride=128), :] = rbuf[d, pl.ds(0, FIELDS), :]
            if extra:
                f, ez, ey = extra
                pad[pl.ds(f * 128 + spot(zg + ez, yg + ey), 1), :] = rbuf[d, pl.ds(FIELDS, 1), :]

        def copy_rows(zs, ys):
            pad[pl.ds(spot(zg, yg), FIELDS, stride=128), :] = pad[
                pl.ds(spot(zs, ys), FIELDS, stride=128), :
            ]

        @pl.when(jnp.logical_not(has_z[-dz]))
        def _():
            copy_rows(zc, yg)
            if extra:
                f, ez, ey = extra
                pad[pl.ds(f * 128 + spot(zg + ez, yg + ey), 1), :] = pad[
                    pl.ds(f * 128 + spot(zc, yg + ey), 1), :
                ]

        @pl.when(jnp.logical_and(has_z[-dz], jnp.logical_not(has_y[-dy])))
        def _():
            copy_rows(zg, yc)
            if extra:
                f, ez, ey = extra
                pad[pl.ds(f * 128 + spot(zg + ez, yg + ey), 1), :] = pad[
                    pl.ds(f * 128 + spot(zg + ez, yc), 1), :
                ]

    for f in range(FIELDS):
        ext[pl.ds(f * tall + 8, nx), :] = pad[pl.ds(f * 128, 128), :].T
    xsend[pl.ds(0, FIELDS), :] = ext[pl.ds(8, FIELDS, stride=tall), :]
    xsend[pl.ds(FIELDS, 1), :] = ext[pl.ds(FX * tall + 9, 1), :]
    xsend[pl.ds(16, FIELDS), :] = ext[pl.ds(7 + nx, FIELDS, stride=tall), :]

    to_left = pltpu.make_async_remote_copy(
        src_ref=xsend.at[pl.ds(0, 16)],
        dst_ref=xrecv.at[pl.ds(0, 16)],
        send_sem=send_sem.at[8],
        recv_sem=recv_sem.at[8],
        device_id={"gx": left},
        device_id_type=MESH,
    )
    to_right = pltpu.make_async_remote_copy(
        src_ref=xsend.at[pl.ds(16, 8)],
        dst_ref=xrecv.at[pl.ds(16, 8)],
        send_sem=send_sem.at[9],
        recv_sem=recv_sem.at[9],
        device_id={"gx": right},
        device_id_type=MESH,
    )
    lane = lax.broadcasted_iota(jnp.int32, (8, 128), 1)
    slab = iz * nz - 1
    zglobal = jnp.zeros((8, 128), jnp.int32) + slab
    for j in range(1, nz + 3):
        zglobal = zglobal + (lane >= j * wide).astype(jnp.int32)
    height = (2 * zglobal + 1 - nz * gz).astype(jnp.float32) * (1.0 / (nz * gz))
    pull = -gravity * courant * height
    to_left.start()
    to_right.start()

    def up(values, axis):
        return pltpu.roll(values, 128 - (wide if axis == 0 else 1), 1)

    def down(values, axis):
        return pltpu.roll(values, wide if axis == 0 else 1, 1)

    def chunk(k):
        r = 7 + 8 * k
        now = [ext[pl.ds(f * tall + r, 8), :] for f in range(FIELDS)]
        below = [ext[pl.ds(f * tall + r - 1, 8), :] for f in range(7)]
        rho, vel, pre, faces = now[0], now[1:4], now[4], now[5:8]
        centre = [
            0.5 * (faces[0] + up(faces[0], 0)),
            0.5 * (faces[1] + up(faces[1], 1)),
            0.5 * (faces[2] + ext[pl.ds(FX * tall + r + 1, 8), :]),
        ]
        cell = cell_terms(rho, vel, pre)
        fluxes = []
        for axis in range(3):
            if axis == 2:
                lrho, lvel, lpre = below[0], below[1:4], below[4]
                lcell = cell_terms(lrho, lvel, lpre)
                lmag = [
                    0.5 * (below[5] + up(below[5], 0)),
                    0.5 * (below[6] + up(below[6], 1)),
                    faces[2],
                ]
            else:
                lrho, lpre = down(rho, axis), down(pre, axis)
                lvel = [down(v, axis) for v in vel]
                lcell = (
                    lrho, down(cell[1], axis), down(cell[2], axis), down(cell[3], axis),
                    [lrho * v for v in lvel],
                )
                lmag = [faces[c] if c == axis else down(centre[c], axis) for c in range(3)]
            umag = [faces[c] if c == axis else centre[c] for c in range(3)]
            lower = state_terms(lcell, lvel, lpre, lmag, axis)
            upper = state_terms(cell, vel, pre, umag, axis)
            fluxes.append(hll(lower, upper, axis))
        squared = centre[0] * centre[0] + centre[1] * centre[1] + centre[2] * centre[2]
        base = [rho] + list(cell[4]) + [cell[3] + 0.5 * squared]
        fz, fy, fx = fluxes
        out = pl.ds(8 * k, 8)
        for m in range(5):
            change = up(fz[m], 0) - fz[m] + up(fy[m], 1) - fy[m]
            value = base[m] - courant * change
            if m == 1:
                value = value + rho * pull
            if m == 4:
                value = value + cell[4][0] * pull
            part[m, out, :] = value
            part[5 + m, out, :] = fx[m]
        part[10, out, :] = 0.25 * (fz[5] + down(fz[5], 1) - fy[5] - down(fy[5], 0))
        part[11, out, :] = fx[5] + down(fx[5], 0) - fz[6]
        part[12, out, :] = fz[6]
        part[13, out, :] = fy[6] - fx[6] - down(fx[6], 1)
        part[14, out, :] = fy[6]

    count = nx // 8
    def body(k, carry):
        chunk(k)
        return carry

    lax.fori_loop(1, count, body, 0, unroll=3)
    def finish(k):
        at = 8 * k
        here, after, before = pl.ds(at + 1, 8), pl.ds(at + 2, 8), pl.ds(at, 8)
        for m in range(5):
            res[m, before, :] = part[m, here, :] - courant * (part[5 + m, after, :] - part[5 + m, here, :])
        ex = part[10, here, :]
        ey = 0.25 * (part[11, here, :] - part[12, before, :])
        ez = 0.25 * (part[13, here, :] + part[14, before, :])
        ey_next = 0.25 * (part[11, after, :] - part[12, here, :])
        ez_next = 0.25 * (part[13, after, :] + part[14, here, :])
        res[7, before, :] = ext[pl.ds(FX * tall + at + 8, 8), :] - courant * ((up(ez, 1) - ez) - (up(ey, 0) - ey))
        res[6, before, :] = ext[pl.ds(FY * tall + at + 8, 8), :] - courant * ((up(ex, 0) - ex) - (ez_next - ez))
        res[5, before, :] = ext[pl.ds(FZ * tall + at + 8, 8), :] - courant * ((ey_next - ey) - (up(ex, 1) - ex))

    for k in range(1, count - 1):
        finish(k)
    to_left.wait_recv()
    to_right.wait_recv()
    ext[pl.ds(8 + nx, FIELDS, stride=tall), :] = xrecv[pl.ds(0, FIELDS), :]
    ext[pl.ds(FX * tall + 9 + nx, 1), :] = xrecv[pl.ds(FIELDS, 1), :]
    ext[pl.ds(7, FIELDS, stride=tall), :] = xrecv[pl.ds(16, FIELDS), :]
    chunk(0)
    chunk(count)

    finish(0)
    finish(count - 1)
    for d in range(8):
        @pl.when(exists(*DIRS[d]))
        def _():
            message(d).wait_send()
    to_left.wait_send()
    to_right.wait_send()


def unpack_kernel(sizes, res, cons_ref, face_ref, turned, out, sem):
    nz, ny = sizes
    plane, wide = nz * ny, ny + 3
    copies = []
    for m in range(FIELDS):
        turned[m] = res[m].T
        for z in range(nz):
            out[pl.ds(m * plane + z * ny, ny), :] = turned[m, pl.ds((z + 1) * wide + 1, ny), :]
        target, base = (cons_ref, m * plane) if m < 5 else (face_ref, (m - 5) * plane)
        copies.append(pltpu.make_async_copy(
            out.at[pl.ds(m * plane, plane)], target.at[pl.ds(base, plane)], sem.at[m]
        ))
        copies[-1].start()
    for copy in copies:
        copy.wait()


def on_device(sizes, density, velocity, pressure, field, corona):
    nz, ny, nx = density.shape
    gz, gy, gx = sizes
    plane = nz * ny
    hbm = pl.BlockSpec(memory_space=pltpu.HBM)
    vmem = pl.BlockSpec(memory_space=pltpu.VMEM)
    f32 = jnp.float32
    rows = FIELDS * max(nz, ny) + max(nz, ny)
    result = pl.pallas_call(
        functools.partial(kernel, (nz, ny, nx, gz, gy, gx)),
        out_shape=pltpu.VMEM((FIELDS, nx, 128), f32),
        in_specs=[hbm] * 5,
        out_specs=vmem,
        scratch_shapes=[
            pltpu.VMEM((FIELDS * plane, nx), f32),
            pltpu.VMEM((plane, nx), f32),
            pltpu.SMEM(corona.shape, jnp.int32),
            pltpu.VMEM((8, rows, nx), f32),
            pltpu.VMEM((8, rows, nx), f32),
            pltpu.VMEM((FIELDS * 128, nx), f32),
            pltpu.VMEM((FIELDS * (nx + 16), 128), f32),
            pltpu.VMEM((24, 128), f32),
            pltpu.VMEM((24, 128), f32),
            pltpu.VMEM((PARTS, nx + 8, 128), f32),
            pltpu.SemaphoreType.DMA((5,)),
            pltpu.SemaphoreType.DMA((10,)),
            pltpu.SemaphoreType.DMA((10,)),
        ],
        compiler_params=pltpu.CompilerParams(
            collective_id=0, has_side_effects=True, vmem_limit_bytes=16 << 20
        ),
    )(
        *(
            pltpu.with_memory_space_constraint(x, pltpu.HBM)
            for x in (
                density.reshape(plane, nx),
                velocity.reshape(3 * plane, nx),
                pressure.reshape(plane, nx),
                field.reshape(3 * plane, nx),
                corona,
            )
        )
    )
    conserved, faces = pl.pallas_call(
        functools.partial(unpack_kernel, (nz, ny)),
        out_shape=(
            jax.ShapeDtypeStruct((5 * plane, nx), f32),
            jax.ShapeDtypeStruct((3 * plane, nx), f32),
        ),
        in_specs=[vmem],
        out_specs=(hbm, hbm),
        scratch_shapes=[
            pltpu.VMEM((FIELDS, 128, nx), f32),
            pltpu.VMEM((FIELDS * plane, nx), f32),
            pltpu.SemaphoreType.DMA((FIELDS,)),
        ],
        compiler_params=pltpu.CompilerParams(vmem_limit_bytes=16 << 20),
    )(result)
    return conserved.reshape(5, nz, ny, nx), faces.reshape(3, nz, ny, nx)


def solution(mesh):
    sizes = tuple(mesh.shape[axis] for axis in ("gz", "gy", "gx"))
    return jax.shard_map(
        functools.partial(on_device, sizes),
        mesh=mesh,
        in_specs=(
            P("gz", "gy", "gx"),
            P(None, "gz", "gy", "gx"),
            P("gz", "gy", "gx"),
            P(None, "gz", "gy", "gx"),
            P(),
        ),
        out_specs=(P(None, "gz", "gy", "gx"), P(None, "gz", "gy", "gx")),
        check_vma=False,
    )
```
